32 devices in a mesh: row: 8 (over y, x, core), col: 4 (over z).
Axes of the slice: x: 2, y: 2, z: 4, core: 2. Of those that a mesh axis runs over, the one named last changes fastest.
Arguments:
- stored_blocks: bfloat16 [8, 4, 64, 128, 128], P('row', 'col'), may hold values from -1 to 1
- stored_ids: int32 [8, 4, 3, 64], P('row', 'col'), may hold values from 0 to 127, as said below
- slab_blocks: bfloat16 [8, 4, 32, 128, 128], P('row', 'col'), may hold values from -1 to 1
- slab_ids: int32 [8, 4, 3, 32], P('row', 'col'), may hold values from 0 to 127, as said below
- pair_lists: int32 [8, 4, 4, 3, 256], P('row', 'col'), may hold values from 0 to 127, as said below
Outputs:
- product: bfloat16 [16384, 1024], P('row', 'col')
The draws below stay inside these ranges and needn't reach their ends.
Inputs may be any that keep to these rules, and one draw needn't show every extreme that they name: `stored_ids`: present slots of cell (r, c) hold blocks of the panel pair made of panels r and r xor c: row index in the lower of the two panels (panel p covers block rows p * 16 to (p + 1) * 16 - 1), column index in the higher, row <= column. Every stored block lies in exactly one slot over all cells. Flags are 0 or 1; a half has at most 64 present slots and some halves have exactly 64. `slab_ids`: the slots of cell (r, c) name each block of panel r xor c and slab columns c * 2 to (c + 1) * 2 - 1 exactly once; flags are 0 or 1, and some cells have all flags 1. pair_lists[r, c, s] names, with flag 1 and ahead of every entry with flag 0, each pair of a present entry of A_s and a present entry of B_s whose column index and row index agree, once each; some list has all 256 flags 1.
All inputs are finite; a program needn't handle non-finite values.
Results may differ from the reference program's by a relative error of at most 0.001.
Values may be sent and summed in bfloat16 or wider, within the bound.
A program may use at most 128 MiB of HBM per device.

```python
import jax
import jax.numpy as jnp
from jax import lax

BLOCK = 128
PANEL = 16
SLAB = 2
STEPS = 4
HALF = 64
SLAB_SLOTS = 32
PAIRS = 256
N_ROW = 8
N_COL = 4


def orient_ids(block_ids, transpose, drop_diag):
    col_ids = jnp.where(transpose, block_ids[0], block_ids[1])
    present = block_ids[2]
    if drop_diag:
        present = present * (block_ids[0] != block_ids[1]).astype(jnp.int32)
    return (col_ids, present)


def layout(key):
    tile_size = PANEL * PANEL
    grid_rows = jnp.arange(N_ROW, dtype=jnp.int32)
    grid_cols = jnp.arange(N_COL, dtype=jnp.int32)

    def stored_half(grid_row, grid_col):
        panel_index = jnp.bitwise_xor(grid_row, grid_col)
        lower = jnp.minimum(grid_row, panel_index)
        upper = jnp.maximum(grid_row, panel_index)
        tile_key = jax.random.fold_in(jax.random.fold_in(key, 11), lower * N_ROW + upper)
        level = jax.random.randint(jax.random.fold_in(tile_key, 1), (), 0, 4)
        lowered = jnp.where(level == 0, 0, jnp.where(level == 3, 2, 1))
        lowered = jnp.where(lower == 0, 0, lowered)
        count = jnp.right_shift(jnp.int32(HALF), lowered.astype(jnp.int32))
        places = jnp.arange(tile_size, dtype=jnp.int32)
        local_row = places // PANEL
        local_col = places % PANEL
        eligible = jnp.where(lower == upper, local_row <= local_col, True)
        ranking = jax.random.permutation(jax.random.fold_in(tile_key, 2), tile_size).astype(jnp.int32)
        scores = jnp.where(eligible, tile_size, 0).astype(jnp.int32) + ranking
        ordered = jnp.argsort(-scores, stable=True).astype(jnp.int32)
        start = jnp.where((grid_row == upper) & (lower != upper), count, 0)
        picks = jnp.take(ordered, start + jnp.arange(HALF, dtype=jnp.int32))
        present = (jnp.arange(HALF, dtype=jnp.int32) < count).astype(jnp.int32)
        device_key = jax.random.fold_in(jax.random.fold_in(key, 13), grid_row * N_COL + grid_col)
        slot_order = jax.random.permutation(device_key, HALF)
        picks = picks[slot_order]
        present = present[slot_order]
        global_row = lower * PANEL + picks // PANEL
        global_col = upper * PANEL + picks % PANEL
        return jnp.stack([global_row, global_col, present]).astype(jnp.int32)
    stored_ids = jax.vmap(jax.vmap(stored_half, (None, 0)), (0, None))(grid_rows, grid_cols)

    def slab_tile(grid_row, grid_col):
        panel_index = jnp.bitwise_xor(grid_row, grid_col)
        device_key = jax.random.fold_in(jax.random.fold_in(key, 17), grid_row * N_COL + grid_col)
        places = jnp.arange(SLAB_SLOTS, dtype=jnp.int32)
        keeping = jax.random.randint(jax.random.fold_in(device_key, 1), (SLAB_SLOTS,), 0, 4) > 0
        keeping = keeping | (grid_row == 0)
        slot_order = jax.random.permutation(jax.random.fold_in(device_key, 2), SLAB_SLOTS)
        places = places[slot_order]
        keeping = keeping[slot_order]
        global_row = panel_index * PANEL + places // SLAB
        global_col = grid_col * SLAB + places % SLAB
        return jnp.stack([global_row, global_col, keeping.astype(jnp.int32)]).astype(jnp.int32)
    slab_ids = jax.vmap(jax.vmap(slab_tile, (None, 0)), (0, None))(grid_rows, grid_cols)
    candidates = 2 * HALF * SLAB_SLOTS
    stride_len = N_COL // STEPS

    def pair_list(grid_row, grid_col, offset):
        moved = offset * stride_len
        source = jnp.bitwise_xor(grid_col, moved)
        panel_index = jnp.bitwise_xor(grid_row, source)
        first_cols, first_present = orient_ids(stored_ids[grid_row, source], grid_row > panel_index, False)
        second_cols, second_present = orient_ids(stored_ids[panel_index, source], grid_row >= panel_index, True)
        left_cols = jnp.concatenate([first_cols, second_cols], 0)
        left_present = jnp.concatenate([first_present, second_present], 0)
        right_ids = slab_ids[jnp.bitwise_xor(grid_row, moved), grid_col]
        matching = (left_present[:, None] > 0) & (right_ids[2][None, :] > 0) & (left_cols[:, None] == right_ids[0][None, :])
        flat_match = matching.reshape(-1).astype(jnp.int32)
        list_key = jax.random.fold_in(jax.random.fold_in(key, 19), (grid_row * N_COL + grid_col) * STEPS + offset)
        breaking = jax.random.permutation(list_key, candidates).astype(jnp.int32)
        ordered = jnp.argsort(-(flat_match * candidates + breaking), stable=True).astype(jnp.int32)[:PAIRS]
        return jnp.stack([ordered // SLAB_SLOTS, ordered % SLAB_SLOTS, flat_match[ordered]]).astype(jnp.int32)
    offsets = jnp.arange(STEPS, dtype=jnp.int32)
    pair_lists = jax.vmap(jax.vmap(jax.vmap(pair_list, (None, None, 0)), (None, 0, None)), (0, None, None))(grid_rows, grid_cols, offsets)
    return (stored_ids, slab_ids, pair_lists)


def draw_stored_ids(key, part):
    return layout(key)[0]


def draw_slab_ids(key, part):
    return layout(key)[1]


def draw_pair_lists(key, part):
    return layout(key)[2]


def levels(stream_key, shape, split, smallest, high):
    factor_of = 1.0
    for position, blocks in split:
        steps = jax.random.uniform(jax.random.fold_in(jax.random.fold_in(stream_key, 6), position), (blocks,), jnp.float32, smallest / len(split), high / len(split))
        factor_of = factor_of * jnp.repeat(jnp.exp(steps), shape[position] // blocks).reshape((-1,) + (1,) * (len(shape) - 1 - position))
    return factor_of


def normal_values(own_key, shape, scale, bound, pieces=(), held_as=jnp.bfloat16):
    entries = jax.random.normal(own_key, shape, jnp.float32) * scale
    if len(pieces) > 0:
        entries = levels(own_key, shape, pieces, -0.22, 0.18) * entries
    return jnp.clip(entries, min=-bound, max=bound).astype(held_as)


def setup_inputs(seed: int = 0) -> dict:
    streams_of = jax.random.split(jax.random.key(seed), 6)
    stored_blocks = normal_values(streams_of[0], (N_ROW, N_COL, HALF, BLOCK, BLOCK), 0.16, 1.0, ((0, 8), (1, 4)))
    stored_ids = draw_stored_ids(jax.random.fold_in(streams_of[5], 71), 0)
    slab_blocks = normal_values(streams_of[2], (N_ROW, N_COL, SLAB_SLOTS, BLOCK, BLOCK), 0.16, 1.0, ((0, 8), (1, 4)))
    slab_ids = draw_slab_ids(jax.random.fold_in(streams_of[5], 71), 0)
    pair_lists = draw_pair_lists(jax.random.fold_in(streams_of[5], 71), 0)
    return dict(stored_blocks=stored_blocks, stored_ids=stored_ids, slab_blocks=slab_blocks, slab_ids=slab_ids, pair_lists=pair_lists)


def orient(values, block_ids, transpose, drop_diag):
    turned = jnp.where(transpose, jnp.swapaxes(values, 1, 2), values)
    row_ids = jnp.where(transpose, block_ids[1], block_ids[0])
    present = block_ids[2]
    if drop_diag:
        present = present * (block_ids[0] != block_ids[1]).astype(jnp.int32)
    return turned, row_ids, present


def reference(stored_blocks, stored_ids, slab_blocks, slab_ids, pair_lists):
    cell_count = PANEL * SLAB
    stride_len = N_COL // STEPS

    def one_device(device):
        grid_row = device // N_COL
        grid_col = device % N_COL
        summed = jnp.zeros((cell_count, BLOCK, BLOCK), jnp.float32)
        for offset in range(STEPS):
            moved = offset * stride_len
            source = jnp.bitwise_xor(grid_col, moved)
            panel_index = jnp.bitwise_xor(grid_row, source)
            first_blocks, first_rows, first_present = orient(
                stored_blocks[grid_row, source], stored_ids[grid_row, source], grid_row > panel_index, False)
            second_blocks, second_rows, second_present = orient(
                stored_blocks[panel_index, source], stored_ids[panel_index, source], grid_row >= panel_index, True)
            left_all = jnp.concatenate([first_blocks, second_blocks], 0)
            left_rows = jnp.concatenate([first_rows, second_rows], 0)
            left_present = jnp.concatenate([first_present, second_present], 0)
            slab_row = jnp.bitwise_xor(grid_row, moved)
            right_all = slab_blocks[slab_row, grid_col]
            right_ids = slab_ids[slab_row, grid_col]
            listed = pair_lists[grid_row, grid_col, offset]
            left_slot = listed[0]
            right_slot = listed[1]
            weights = listed[2] * left_present[left_slot] * right_ids[2][right_slot]
            target = (left_rows[left_slot] - grid_row * PANEL) * SLAB + right_ids[1][right_slot] - grid_col * SLAB
            target = jnp.where(weights > 0, target, cell_count).astype(jnp.int32)
            left_blocks = left_all[left_slot].astype(jnp.float32)
            right_blocks = right_all[right_slot].astype(jnp.float32)
            blocks = jnp.einsum("pij,pjk->pik", left_blocks, right_blocks)
            summed = summed + jax.ops.segment_sum(blocks, target, num_segments=cell_count + 1)[:cell_count]
        out_tile = summed.reshape(PANEL, SLAB, BLOCK, BLOCK).transpose(0, 2, 1, 3)
        return out_tile.reshape(PANEL * BLOCK, SLAB * BLOCK).astype(jnp.bfloat16)

    tiles = lax.map(one_device, jnp.arange(N_ROW * N_COL, dtype=jnp.int32))
    tiles = tiles.reshape(N_ROW, N_COL, PANEL * BLOCK, SLAB * BLOCK).transpose(0, 2, 1, 3)
    return tiles.reshape(N_ROW * PANEL * BLOCK, N_COL * SLAB * BLOCK)
```

```python
import functools

import jax
import jax.numpy as jnp
from jax import lax
from jax.experimental import pallas as pl
from jax.experimental.pallas import tpu as pltpu
from jax.sharding import PartitionSpec as P

PANEL = 16
SLAB = 2
STEPS = 4
CHUNKS = 8
MESH = pl.DeviceIdType.MESH


def flipped(value, mask, bits):
    out = value
    for b in range(bits):
        w = 2**b
        out = out + ((mask // w) % 2) * (w - 2 * w * ((value // w) % 2))
    return out


def gather_kernel(
    stride, bits, own, slab, ids, names, out, blocks, slabs, row_ids, pair_ids, slab_ids,
    stage, right_all, acc, table, scalars,
    z_send, z_recv, p_send, p_recv, b_send, b_recv, l_sem, t_sem,
):
    r = lax.axis_index("row")
    c = lax.axis_index("col")
    pos = c // stride
    rem = c % stride
    left = c - stride
    right = c + stride
    slots, edge = own.shape[0], own.shape[1]
    size = slots // CHUNKS
    slab_slots = slab.shape[0]

    def partner(s):
        return flipped(r, s * stride + rem, bits)

    def shifted(t):
        return flipped(r, t * stride, bits)

    bar = pltpu.get_barrier_semaphore()

    def greet(row, col):
        pl.semaphore_signal(bar, inc=1, device_id=(row, col), device_id_type=MESH)

    def cond_kind(s):
        return s * stride + rem > 0

    @pl.when(pos > 0)
    def _():
        greet(r, left)

    @pl.when(pos < STEPS - 1)
    def _():
        greet(r, right)

    for s in range(STEPS):
        @pl.when(cond_kind(s))
        def _():
            greet(partner(s), c)
    for t in range(1, STEPS):
        greet(shifted(t), c)

    ends = jnp.minimum(pos, 1) + jnp.minimum(STEPS - 1 - pos, 1)
    pl.semaphore_wait(bar, ends + jnp.minimum(rem, 1) + 2 * (STEPS - 1))

    def piece(ref, id_ref, ch):
        return id_ref if ch == 0 else ref.at[pl.ds((ch - 1) * size, size)]

    def landed(s, ch):
        return row_ids.at[s] if ch == 0 else blocks.at[s, pl.ds(1 + (ch - 1) * size, size)]

    def paired(s, ch):
        return pair_ids.at[s] if ch == 0 else blocks.at[s, pl.ds(1 + slots + (ch - 1) * size, size)]

    def along(src, s, ch, way):
        return pltpu.make_async_remote_copy(
            src_ref=src, dst_ref=landed(s, ch), send_sem=z_send.at[way, s, ch],
            recv_sem=z_recv.at[s, ch], device_id=(r, right if way else left), device_id_type=MESH)

    def across(src, s, ch):
        return pltpu.make_async_remote_copy(
            src_ref=src, dst_ref=paired(s, ch), send_sem=p_send.at[s, ch],
            recv_sem=p_recv.at[s, ch], device_id=(partner(s), c), device_id_type=MESH)

    def slab_copy(src, t, to, what):
        dst = slab_ids.at[t] if what == 0 else slabs.at[t, pl.ds(1, slab_slots)]
        return pltpu.make_async_remote_copy(
            src_ref=src, dst_ref=dst, send_sem=b_send.at[t, what],
            recv_sem=b_recv.at[t, what], device_id=(shifted(to), c), device_id_type=MESH)

    pieces = range(CHUNKS + 1)
    kept = 1 + CHUNKS // 2
    for ch in pieces:
        mine = piece(own, ids, ch)

        @pl.when(pos > (1 if ch >= kept else 0))
        def _():
            along(mine, pos, ch, 0).start()

        @pl.when(pos < STEPS - 1)
        def _():
            along(mine, pos, ch, 1).start()

        @pl.when(cond_kind(pos))
        def _():
            across(mine, pos, ch).start()
        if ch == 0:
            for what, src in ((0, names), (1, slab)):
                slab_copy(src, 2, 2, what).start()
                slab_copy(src, 1, 1, what).start()
    local = (
        pltpu.make_async_copy(own, blocks.at[pos, pl.ds(1, slots)], l_sem.at[0]),
        pltpu.make_async_copy(ids, row_ids.at[pos], l_sem.at[1]),
        pltpu.make_async_copy(slab, slabs.at[0, pl.ds(1, slab_slots)], l_sem.at[2]),
        pltpu.make_async_copy(names, slab_ids.at[0], l_sem.at[3]),
    )
    for copy in local:
        copy.start()

    zero_block = jnp.zeros((edge, edge), blocks.dtype)
    for s in range(STEPS):
        slabs[s, 0] = zero_block
        stage[s, 0] = zero_block

    def inverted(at_row, at_col, present, base, rows):
        count = at_row.shape[1]
        sub = lax.broadcasted_iota(jnp.int32, (PANEL, count), 0)
        first = lax.broadcasted_iota(jnp.int32, (1, count), 1)
        lane = lax.broadcasted_iota(jnp.int32, (PANEL, 128), 1)
        value = jnp.where(present, first + (1 + base), 0)
        hit = jnp.where(at_col == sub, value, 0)
        found = jnp.zeros((PANEL, 128), jnp.int32)
        for a in range(rows):
            most = jnp.max(jnp.where(at_row == a, hit, 0), axis=1, keepdims=True)
            found = jnp.where(lane == a, most, found)
        return found

    def prepare(s):
        q = partner(s)
        low, high = jnp.minimum(r, q) * PANEL, jnp.maximum(r, q) * PANEL
        t = flipped(s, pos, 2)

        def part(ref, base, turn):
            i, j = ref[s, 0] - low, ref[s, 1] - high
            keep = ref[s, 2] > 0
            return inverted(j if turn else i, i if turn else j, keep, base, PANEL)

        @pl.when(r < q)
        def _():
            table[0:PANEL] = jnp.maximum(part(row_ids, 0, False), part(pair_ids, slots, False))

        @pl.when(r > q)
        def _():
            table[0:PANEL] = jnp.maximum(part(row_ids, 0, True), part(pair_ids, slots, True))

        @pl.when(r == q)
        def _():
            i, j = row_ids[s, 0] - low, row_ids[s, 1] - high
            keep = row_ids[s, 2] > 0
            off = jnp.logical_and(keep, i != j)
            table[0:PANEL] = jnp.maximum(
                inverted(i, j, keep, 0, PANEL), inverted(j, i, off, slots, PANEL))

        table[PANEL:] = inverted(
            slab_ids[t, 1] - c * SLAB, slab_ids[t, 0] - q * PANEL, slab_ids[t, 2] > 0, 0, SLAB)
        fetch = pltpu.make_async_copy(table, scalars.at[s], t_sem.at[0])
        fetch.start()
        fetch.wait()

        def slab_row(k, carry):
            for n in range(SLAB):
                right_all[s, k, :, n * edge : (n + 1) * edge] = slabs[t, scalars[s, PANEL + k, n]]
            return carry

        lax.fori_loop(0, PANEL, slab_row, 0)

    def move(s, to, of, turn):
        def some(g, carry):
            for x in range(4):
                block = blocks[s, of + g * 4 + x]
                stage[s, to + g * 4 + x] = block.T if turn else block
            return carry

        lax.fori_loop(0, size // 4, some, 0)

    def hold(s, at):
        turned = r > partner(s)

        @pl.when(turned)
        def _():
            move(s, at, at, True)

        @pl.when(jnp.logical_not(turned))
        def _():
            move(s, at, at, False)

    def hold_row(s, ch):
        at = 1 + (ch - 1) * size
        hold(s, at)

        @pl.when(jnp.logical_not(cond_kind(s)))
        def _():
            move(s, slots + at, at, True)

    def hold_pair(s, ch):
        @pl.when(cond_kind(s))
        def _():
            hold(s, 1 + slots + (ch - 1) * size)

    depth = PANEL * edge
    group = 4

    def multiply(s, first, final):
        slab_full = right_all[s].reshape(depth, SLAB * edge)

        def product(g, carry):
            rows = []
            for a in range(group):
                i = g * group + a
                rows.append(jnp.concatenate(
                    [stage[s, scalars[s, j, i]] for j in range(PANEL)], axis=1))
            at = pl.multiple_of(g * group * edge, group * edge)
            total = jnp.dot(
                jnp.concatenate(rows, axis=0), slab_full, preferred_element_type=jnp.float32)
            if not first:
                total = total + acc[pl.ds(at, group * edge)]
            if final:
                out[pl.ds(at, group * edge)] = total.astype(out.dtype)
            else:
                acc[pl.ds(at, group * edge)] = total
            return carry

        lax.fori_loop(0, PANEL // group, product, 0)

    second = jnp.where(pos == 2, 1, 2)
    last = jnp.where(pos == 0, 1, jnp.where(pos == 1, 3, 0))
    third = 6 - pos - second - last

    def crossed(s, ch):
        @pl.when(cond_kind(s))
        def _():
            across(landed(s, ch), s, ch).wait_recv()

    def take(s, first=False):
        crossed(s, 0)
        prepare(s)
        for ch in range(1, CHUNKS + 1):
            hold_row(s, ch)
            crossed(s, ch)
            hold_pair(s, ch)
        multiply(s, first, False)

    for d in range(1, STEPS):
        for ch in pieces:
            for way in (1, 0):
                s = pos - d if way else pos + d
                here = s >= 0 if way else s <= STEPS - 1
                if d == 1 and not way and ch >= kept:
                    here = jnp.logical_and(here, pos > 0)
                more = pos < STEPS - 1 if way else pos > 0

                @pl.when(here)
                def _():
                    along(landed(s, ch), s, ch, way).wait_recv()

                    @pl.when(more)
                    def _():
                        along(landed(s, ch), s, ch, way).start()

                    @pl.when(cond_kind(s))
                    def _():
                        across(landed(s, ch), s, ch).start()
            if d == 1 and ch == 1:
                for what, src in ((0, slab_ids.at[2]), (1, slabs.at[2, pl.ds(1, slab_slots)])):
                    slab_copy(src, 2, 2, what).wait_recv()
                    slab_copy(src, 3, 1, what).start()

        if d == 1:
            for copy in local:
                copy.wait()
            for what, src in ((0, names), (1, slab)):
                slab_copy(src, 1, 1, what).wait()
                slab_copy(src, 2, 2, what).wait_send()
                slab_copy(src, 3, 1, what).wait()
            take(pos, True)
        if d == 2:
            @pl.when(pos == 1)
            def _():
                for ch in range(kept, CHUNKS + 1):
                    along(piece(own, ids, ch), pos, ch, 0).start()

            take(second)
    take(third)

    crossed(last, 0)
    prepare(last)
    for ch in range(1, CHUNKS + 1):
        if ch >= kept:
            @pl.when(pos == 0)
            def _():
                along(landed(1, ch), 1, ch, 0).wait_recv()
                across(landed(1, ch), 1, ch).start()

        hold_row(last, ch)
        crossed(last, ch)
        hold_pair(last, ch)
    multiply(last, False, True)
    for s in range(STEPS):
        for ch in pieces:
            @pl.when(cond_kind(s))
            def _():
                across(landed(s, ch), s, ch).wait_send()

            @pl.when(jnp.logical_and(s <= pos, pos < STEPS - 1))
            def _():
                along(landed(s, ch), s, ch, 1).wait_send()

            @pl.when(jnp.logical_and(s >= pos, pos > 0))
            def _():
                along(landed(s, ch), s, ch, 0).wait_send()


def gather(own, slab, ids, names, stride, bits):
    any_spec = pl.BlockSpec(memory_space=pl.ANY)
    dma = pltpu.SemaphoreType.DMA
    slots, edge = own.shape[0], own.shape[1]
    tile = (PANEL * edge, SLAB * edge)
    listed = pltpu.VMEM((STEPS,) + ids.shape, ids.dtype)
    return pl.pallas_call(
        functools.partial(gather_kernel, stride, bits),
        out_shape=jax.ShapeDtypeStruct(tile, own.dtype),
        in_specs=[any_spec] * 4,
        out_specs=pl.BlockSpec(memory_space=pltpu.VMEM),
        scratch_shapes=[
            pltpu.VMEM((STEPS, 2 * slots + 1, edge, edge), own.dtype),
            pltpu.VMEM((STEPS, slab.shape[0] + 1, edge, edge), own.dtype),
            listed, listed, pltpu.VMEM((STEPS,) + names.shape, names.dtype),
            pltpu.VMEM((STEPS, 2 * slots + 1, edge, edge), own.dtype),
            pltpu.VMEM((STEPS, PANEL, edge, SLAB * edge), own.dtype),
            pltpu.VMEM(tile, jnp.float32),
            pltpu.VMEM((2 * PANEL, 128), jnp.int32),
            pltpu.SMEM((STEPS, 2 * PANEL, 128), jnp.int32),
            dma((2, STEPS, CHUNKS + 1)), dma((STEPS, CHUNKS + 1)),
            dma((STEPS, CHUNKS + 1)), dma((STEPS, CHUNKS + 1)),
            dma((STEPS, 2)), dma((STEPS, 2)), dma((4,)), dma((1,)),
        ],
        compiler_params=pltpu.CompilerParams(
            collective_id=0, has_side_effects=True, vmem_limit_bytes=56 * 2**20
        ),
    )(own, slab, ids, names)


def on_device(stored_blocks, stored_ids, slab_blocks, slab_ids, pair_lists):
    stride = lax.axis_size("col") // STEPS
    bits = lax.axis_size("row").bit_length() - 1
    ids = stored_ids.reshape(stored_ids.shape[2], 1, stored_ids.shape[3])
    names = slab_ids.reshape(slab_ids.shape[2], 1, slab_ids.shape[3])
    return gather(stored_blocks[0, 0], slab_blocks[0, 0], ids, names, stride, bits)


def solution(mesh):
    return jax.shard_map(
        on_device,
        mesh=mesh,
        in_specs=(
            P("row", "col", None, None, None),
            P("row", "col", None, None),
            P("row", "col", None, None, None),
            P("row", "col", None, None),
            P("row", "col", None, None, None),
        ),
        out_specs=P("row", "col"),
        check_vma=False,
    )
```

```python
import functools

import jax
import jax.numpy as jnp
from jax import lax
from jax.experimental import pallas as pl
from jax.experimental.pallas import tpu as pltpu
from jax.sharding import PartitionSpec as P

PANEL = 16
SLAB = 2
STEPS = 4
CHUNKS = 8
FORWARDED = 2
GROUPS = 4
MESH = pl.DeviceIdType.MESH


def flipped(value, mask, bits):
    out = value
    for b in range(bits):
        w = 2**b
        out = out + ((mask // w) % 2) * (w - 2 * w * ((value // w) % 2))
    return out


def product_kernel(
    stride, bits, own, slab, ids, names, out, blocks, slabs, row_ids, pair_ids, slab_ids,
    stage, right_all, acc, result, table, scalars,
    z_send, z_recv, p_send, p_recv, f_send, b_send, b_recv, o_send, o_recv, l_sem, t_sem,
):
    r = lax.axis_index("row")
    c = lax.axis_index("col")
    pos = c // stride
    rem = c % stride
    slots, edge = own.shape[0], own.shape[1]
    size = slots // CHUNKS
    slab_slots = slab.shape[0]
    width = SLAB * edge
    worker = jnp.logical_and(pos > 0, pos < STEPS - 1)
    low_side = pos < STEPS // 2
    ahead = jnp.where(low_side, c + stride, c - stride)
    behind = jnp.where(low_side, c - stride, c + stride)
    fed = jnp.where(low_side, 0, STEPS - 1)
    near = STEPS - 1 - pos
    far = STEPS - 1 - fed
    fed_col = jnp.where(worker, behind, c)

    def partner(s):
        return flipped(r, s * stride + rem, bits)

    def shifted(t):
        return flipped(r, t * stride, bits)

    bar = pltpu.get_barrier_semaphore()

    def greet(row, col):
        pl.semaphore_signal(bar, inc=1, device_id=(row, col), device_id_type=MESH)

    def cond_kind(s):
        return s * stride + rem > 0

    greet(r, ahead)
    greet(shifted(2), c)

    @pl.when(worker)
    def _():
        greet(r, behind)
        greet(shifted(1), c)
        for s in range(STEPS):
            @pl.when(cond_kind(s))
            def _():
                greet(partner(s), c)

    @pl.when(pos == STEPS - 1)
    def _():
        greet(partner(STEPS - 1), c)

    @pl.when(worker)
    def _():
        pl.semaphore_wait(bar, 4 + (STEPS - 1) + jnp.minimum(rem, 1))

    @pl.when(pos == STEPS - 1)
    def _():
        pl.semaphore_wait(bar, 3)

    @pl.when(pos == 0)
    def _():
        pl.semaphore_wait(bar, 2)

    pieces = range(CHUNKS + 1)
    tail = range(CHUNKS + 1 - FORWARDED, CHUNKS + 1)

    def span(ch):
        return pl.ds((ch - 1) * size, size)

    def mine(ch):
        return ids if ch == 0 else own.at[span(ch)]

    def landed(s, ch):
        return row_ids.at[s] if ch == 0 else blocks.at[s, span(ch)]

    def paired(s, ch):
        return pair_ids.at[s] if ch == 0 else blocks.at[s, pl.ds(slots + (ch - 1) * size, size)]

    def along(src, s, ch):
        return pltpu.make_async_remote_copy(
            src_ref=src, dst_ref=landed(s, ch), send_sem=z_send.at[s, ch],
            recv_sem=z_recv.at[s, ch], device_id=(r, ahead), device_id_type=MESH)

    def across(src, s, ch):
        return pltpu.make_async_remote_copy(
            src_ref=src, dst_ref=paired(s, ch), send_sem=p_send.at[s, ch],
            recv_sem=p_recv.at[s, ch], device_id=(partner(s), c), device_id_type=MESH)

    def forward(ch):
        return pltpu.make_async_remote_copy(
            src_ref=paired(pos, ch), dst_ref=paired(pos, ch), send_sem=f_send.at[ch],
            recv_sem=p_recv.at[pos, ch], device_id=(r, ahead), device_id_type=MESH)

    def tile(side, t, what):
        return slab_ids.at[side, t] if what == 0 else slabs.at[side, t, pl.ds(1, slab_slots)]

    def slab_copy(src, side, t, what, to):
        return pltpu.make_async_remote_copy(
            src_ref=src, dst_ref=tile(side, t, what), send_sem=b_send.at[side, t, what],
            recv_sem=b_recv.at[side, t, what], device_id=to, device_id_type=MESH)

    def give(side, t, to, srcs):
        for what in range(2):
            slab_copy(srcs[what], side, t, what, to).start()

    def have(side, t):
        for what in range(2):
            slab_copy(tile(side, t, what), side, t, what, (r, c)).wait_recv()

    def gave(side, t):
        for what in range(2):
            slab_copy(tile(side, t, what), side, t, what, (r, c)).wait_send()

    def tiles(side, t):
        return tile(side, t, 0), tile(side, t, 1)

    block_rows = PANEL // GROUPS

    def returned(g):
        at = pl.ds(pl.multiple_of(g * block_rows * edge, block_rows * edge), block_rows * edge)
        return pltpu.make_async_remote_copy(
            src_ref=result.at[at], dst_ref=result.at[at], send_sem=o_send.at[g],
            recv_sem=o_recv.at[g], device_id=(r, behind), device_id_type=MESH)

    def got(g):
        at = pl.ds(pl.multiple_of(g * block_rows * edge, block_rows * edge), block_rows * edge)
        return pltpu.make_async_remote_copy(
            src_ref=result.at[at], dst_ref=result.at[at], send_sem=o_send.at[g],
            recv_sem=o_recv.at[g], device_id=(r, ahead), device_id_type=MESH)

    plane_two = (shifted(2), c)
    plane_one = (shifted(1), c)
    inward = (r, ahead)
    give(0, 2, plane_two, (names, slab))

    @pl.when(jnp.logical_not(worker))
    def _():
        give(1, 0, inward, (names, slab))
        for ch in range(3):
            along(mine(ch), pos, ch).start()

        @pl.when(pos > 0)
        def _():
            for ch in tail:
                across(mine(ch), pos, ch).start()

        have(0, 2)
        give(1, 2, inward, tiles(0, 2))
        for ch in range(3, CHUNKS + 1):
            along(mine(ch), pos, ch).start()

        @pl.when(pos > 0)
        def _():
            for ch in tail:
                across(mine(ch), pos, ch).wait_recv()
                forward(ch).start()

        for g in range(GROUPS):
            got(g).wait_recv()
            at = pl.ds(g * block_rows * edge, block_rows * edge)
            out[at] = result[at]
        gave(0, 2)
        gave(1, 0)
        gave(1, 2)
        for ch in pieces:
            along(mine(ch), pos, ch).wait_send()

        @pl.when(pos > 0)
        def _():
            for ch in tail:
                across(mine(ch), pos, ch).wait_send()
                forward(ch).wait_send()

    def held_back(s, ch):
        return s == pos + 1 if ch in tail else False

    def send_across(src, s, ch):
        @pl.when(jnp.logical_and(cond_kind(s), jnp.logical_not(held_back(s, ch))))
        def _():
            across(src, s, ch).start()

    def crossed(s, ch):
        waits = cond_kind(s)
        if s == 2 and ch in tail:
            waits = jnp.logical_and(waits, pos != 2)

        @pl.when(waits)
        def _():
            across(landed(s, ch), s, ch).wait_recv()

    def inverted(at_row, at_col, present, base, rows):
        count = at_row.shape[1]
        sub = lax.broadcasted_iota(jnp.int32, (PANEL, count), 0)
        first = lax.broadcasted_iota(jnp.int32, (1, count), 1)
        lane = lax.broadcasted_iota(jnp.int32, (PANEL, 128), 1)
        value = jnp.where(present, first + (1 + base), 0)
        hit = jnp.where(at_col == sub, value, 0)
        found = jnp.zeros((PANEL, 128), jnp.int32)
        for a in range(rows):
            most = jnp.max(jnp.where(at_row == a, hit, 0), axis=1, keepdims=True)
            found = jnp.where(lane == a, most, found)
        return found

    def prepare(s):
        q = partner(s)
        low, high = jnp.minimum(r, q) * PANEL, jnp.maximum(r, q) * PANEL

        def part(ref, base, turn):
            i, j = ref[s, 0] - low, ref[s, 1] - high
            keep = ref[s, 2] > 0
            return inverted(j if turn else i, i if turn else j, keep, base, PANEL)

        @pl.when(r < q)
        def _():
            table[0:PANEL] = jnp.maximum(part(row_ids, 0, False), part(pair_ids, slots, False))

        @pl.when(r > q)
        def _():
            table[0:PANEL] = jnp.maximum(part(row_ids, 0, True), part(pair_ids, slots, True))

        @pl.when(r == q)
        def _():
            i, j = row_ids[s, 0] - low, row_ids[s, 1] - high
            keep = row_ids[s, 2] > 0
            off = jnp.logical_and(keep, i != j)
            table[0:PANEL] = jnp.maximum(
                inverted(i, j, keep, 0, PANEL), inverted(j, i, off, slots, PANEL))

        places = ((0, flipped(s, pos, 2), c), (1, flipped(s, fed, 2), fed_col))
        for side, t, col in places:
            table[(1 + side) * PANEL : (2 + side) * PANEL] = inverted(
                slab_ids[side, t, 1] - col * SLAB, slab_ids[side, t, 0] - q * PANEL,
                slab_ids[side, t, 2] > 0, 0, SLAB)
        fetch = pltpu.make_async_copy(table, scalars.at[s], t_sem.at[0])
        fetch.start()
        fetch.wait()

        def slab_row(k, carry):
            for side, t, _ in places:
                for n in range(SLAB):
                    at = side * width + n * edge
                    right_all[k, :, at : at + edge] = slabs[
                        side, t, scalars[s, (1 + side) * PANEL + k, n]]
            return carry

        lax.fori_loop(0, PANEL, slab_row, 0)

    def move(s, to, of, turn):
        def some(g, carry):
            for x in range(4):
                block = blocks[s, of + g * 4 + x]
                stage[1 + to + g * 4 + x] = block.T if turn else block
            return carry

        lax.fori_loop(0, size // 4, some, 0)

    def hold(s, at):
        turned = r > partner(s)

        @pl.when(turned)
        def _():
            move(s, at, at, True)

        @pl.when(jnp.logical_not(turned))
        def _():
            move(s, at, at, False)

    def hold_row(s, ch):
        at = (ch - 1) * size
        hold(s, at)

        @pl.when(jnp.logical_not(cond_kind(s)))
        def _():
            move(s, slots + at, at, True)

    def hold_pair(s, ch):
        @pl.when(cond_kind(s))
        def _():
            hold(s, slots + (ch - 1) * size)

    depth = PANEL * edge

    def rows_of(g):
        return pl.ds(pl.multiple_of(g * block_rows * edge, block_rows * edge), block_rows * edge)

    def some_rows(s, g, right):
        rows = []
        for a in range(block_rows):
            rows.append(jnp.concatenate(
                [stage[scalars[s, j, g * block_rows + a]] for j in range(PANEL)], axis=1))
        return jnp.dot(
            jnp.concatenate(rows, axis=0), right, preferred_element_type=jnp.float32)

    def multiply(s, first):
        right = right_all[...].reshape(depth, 2 * width)

        def product(g, carry):
            total = some_rows(s, g, right)
            acc[rows_of(g)] = total if first else total + acc[rows_of(g)]
            return carry

        lax.fori_loop(0, GROUPS, product, 0)

    def take(s, first=False):
        crossed(s, 0)
        prepare(s)
        for ch in range(1, CHUNKS + 1):
            hold_row(s, ch)
            crossed(s, ch)
            hold_pair(s, ch)
        multiply(s, first)

    @pl.when(worker)
    def _():
        give(0, 1, plane_one, (names, slab))
        for ch in pieces:
            along(mine(ch), pos, ch).start()
        for ch in (0, *tail, *range(1, CHUNKS + 1 - FORWARDED)):
            send_across(mine(ch), pos, ch)
        local = (
            pltpu.make_async_copy(own, blocks.at[pos, pl.ds(0, slots)], l_sem.at[0]),
            pltpu.make_async_copy(ids, row_ids.at[pos], l_sem.at[1]),
            pltpu.make_async_copy(slab, slabs.at[0, 0, pl.ds(1, slab_slots)], l_sem.at[2]),
            pltpu.make_async_copy(names, slab_ids.at[0, 0], l_sem.at[3]),
        )
        for copy in local:
            copy.start()
        zero_block = jnp.zeros((edge, edge), blocks.dtype)
        for side in range(2):
            for t in range(STEPS):
                slabs[side, t, 0] = zero_block
        stage[0] = zero_block

        def relay_fed(ch):
            along(landed(fed, ch), fed, ch).wait_recv()
            along(landed(fed, ch), fed, ch).start()
            send_across(landed(fed, ch), fed, ch)

        for ch in pieces:
            along(landed(near, ch), near, ch).wait_recv()
            send_across(landed(near, ch), near, ch)
            if ch == 2:
                have(0, 2)
                give(0, 3, plane_one, tiles(0, 2))
            if ch == 4:
                have(1, 0)
                give(1, 1, plane_one, tiles(1, 0))
            if ch == 6:
                for n in range(3):
                    relay_fed(n)

        @pl.when(pos == 2)
        def _():
            for ch in tail:
                across(landed(pos, ch), pos, ch).wait_recv()
                forward(ch).start()

        have(1, 2)
        give(1, 3, plane_one, tiles(1, 2))
        for copy in local:
            copy.wait()
        have(0, 1)
        have(0, 3)
        have(1, 1)
        have(1, 3)

        take(1, True)
        for ch in pieces:
            if ch > 2:
                relay_fed(ch)
            along(landed(far, ch), far, ch).wait_recv()
            send_across(landed(far, ch), far, ch)
            if ch == 4:
                take(2)
        take(0)
        s = STEPS - 1
        crossed(s, 0)
        prepare(s)
        for ch in range(1, CHUNKS + 1):
            hold_row(s, ch)
            crossed(s, ch)
            hold_pair(s, ch)
        right = right_all[:, :, width:].reshape(depth, width)

        def last_away(g, carry):
            total = some_rows(s, g, right) + acc[rows_of(g), width:]
            result[rows_of(g)] = total.astype(result.dtype)

            @pl.when(g > 0)
            def _():
                returned(g - 1).start()
            return carry

        lax.fori_loop(0, GROUPS, last_away, 0)
        kept = right_all[:, :, :width].reshape(depth, width)

        def last_here(g, carry):
            total = some_rows(s, g, kept) + acc[rows_of(g), :width]
            out[rows_of(g)] = total.astype(out.dtype)

            @pl.when(g == 0)
            def _():
                returned(GROUPS - 1).start()
            return carry

        lax.fori_loop(0, GROUPS, last_here, 0)
        for t in range(1, STEPS):
            gave(0, t)
        gave(1, 1)
        gave(1, 3)
        for ch in pieces:
            for s in range(STEPS):
                @pl.when(jnp.logical_and(cond_kind(s), jnp.logical_not(held_back(s, ch))))
                def _():
                    across(landed(s, ch), s, ch).wait_send()
            along(landed(pos, ch), pos, ch).wait_send()
            along(landed(fed, ch), fed, ch).wait_send()

        @pl.when(pos == 2)
        def _():
            for ch in tail:
                forward(ch).wait_send()

        for g in range(GROUPS):
            returned(g).wait_send()


def product_call(own, slab, ids, names, stride, bits):
    any_spec = pl.BlockSpec(memory_space=pl.ANY)
    dma = pltpu.SemaphoreType.DMA
    slots, edge = own.shape[0], own.shape[1]
    tile = (PANEL * edge, SLAB * edge)
    listed = pltpu.VMEM((STEPS,) + ids.shape, ids.dtype)
    return pl.pallas_call(
        functools.partial(product_kernel, stride, bits),
        out_shape=jax.ShapeDtypeStruct(tile, own.dtype),
        in_specs=[any_spec] * 4,
        out_specs=pl.BlockSpec(memory_space=pltpu.VMEM),
        scratch_shapes=[
            pltpu.VMEM((STEPS, 2 * slots, edge, edge), own.dtype),
            pltpu.VMEM((2, STEPS, slab.shape[0] + 1, edge, edge), own.dtype),
            listed, listed, pltpu.VMEM((2, STEPS) + names.shape, names.dtype),
            pltpu.VMEM((2 * slots + 1, edge, edge), own.dtype),
            pltpu.VMEM((PANEL, edge, 2 * SLAB * edge), own.dtype),
            pltpu.VMEM((PANEL * edge, 2 * SLAB * edge), jnp.float32),
            pltpu.VMEM(tile, own.dtype),
            pltpu.VMEM((3 * PANEL, 128), jnp.int32),
            pltpu.SMEM((STEPS, 3 * PANEL, 128), jnp.int32),
            dma((STEPS, CHUNKS + 1)), dma((STEPS, CHUNKS + 1)),
            dma((STEPS, CHUNKS + 1)), dma((STEPS, CHUNKS + 1)), dma((CHUNKS + 1,)),
            dma((2, STEPS, 2)), dma((2, STEPS, 2)), dma((GROUPS,)), dma((GROUPS,)),
            dma((4,)), dma((1,)),
        ],
        compiler_params=pltpu.CompilerParams(
            collective_id=0, has_side_effects=True, vmem_limit_bytes=56 * 2**20
        ),
    )(own, slab, ids, names)


def on_device(stored_blocks, stored_ids, slab_blocks, slab_ids, pair_lists):
    stride = lax.axis_size("col") // STEPS
    bits = lax.axis_size("row").bit_length() - 1
    ids = stored_ids.reshape(stored_ids.shape[2], 1, stored_ids.shape[3])
    names = slab_ids.reshape(slab_ids.shape[2], 1, slab_ids.shape[3])
    return product_call(stored_blocks[0, 0], slab_blocks[0, 0], ids, names, stride, bits)


def solution(mesh):
    return jax.shard_map(
        on_device,
        mesh=mesh,
        in_specs=(
            P("row", "col", None, None, None),
            P("row", "col", None, None),
            P("row", "col", None, None, None),
            P("row", "col", None, None),
            P("row", "col", None, None, None),
        ),
        out_specs=P("row", "col"),
        check_vma=False,
    )
```

```python
import functools

import jax
import jax.numpy as jnp
from jax import lax
from jax.experimental import pallas as pl
from jax.experimental.pallas import tpu as pltpu
from jax.sharding import PartitionSpec as P

PANEL = 16
SLAB = 2
STEPS = 4
CHUNKS = 8
FORWARDED = 1
GROUPS = 4
MESH = pl.DeviceIdType.MESH


def flipped(value, mask, bits):
    out = value
    for b in range(bits):
        w = 2**b
        out = out + ((mask // w) % 2) * (w - 2 * w * ((value // w) % 2))
    return out


def product_kernel(
    stride, bits, own, slab, ids, names, out, blocks, slabs, row_ids, pair_ids, slab_ids,
    stage, right_all, acc, result, table, scalars,
    z_send, z_recv, p_send, p_recv, f_send, b_send, b_recv, o_send, o_recv, l_sem, t_sem,
):
    r = lax.axis_index("row")
    c = lax.axis_index("col")
    pos = c // stride
    rem = c % stride
    slots, edge = own.shape[0], own.shape[1]
    size = slots // CHUNKS
    slab_slots = slab.shape[0]
    width = SLAB * edge
    worker = jnp.logical_and(pos > 0, pos < STEPS - 1)
    low_side = pos < STEPS // 2
    ahead = jnp.where(low_side, c + stride, c - stride)
    behind = jnp.where(low_side, c - stride, c + stride)
    fed = jnp.where(low_side, 0, STEPS - 1)
    near = STEPS - 1 - pos
    far = STEPS - 1 - fed
    fed_col = jnp.where(worker, behind, c)

    def partner(s):
        return flipped(r, s * stride + rem, bits)

    def shifted(t):
        return flipped(r, t * stride, bits)

    bar = pltpu.get_barrier_semaphore()

    def greet(row, col):
        pl.semaphore_signal(bar, inc=1, device_id=(row, col), device_id_type=MESH)

    def cond_kind(s):
        return s * stride + rem > 0

    greet(r, ahead)
    greet(shifted(2), c)

    @pl.when(worker)
    def _():
        greet(r, behind)
        greet(shifted(1), c)
        for s in range(STEPS):
            @pl.when(cond_kind(s))
            def _():
                greet(partner(s), c)

    @pl.when(pos == STEPS - 1)
    def _():
        greet(partner(STEPS - 1), c)

    @pl.when(worker)
    def _():
        pl.semaphore_wait(bar, 4 + (STEPS - 1) + jnp.minimum(rem, 1))

    @pl.when(pos == STEPS - 1)
    def _():
        pl.semaphore_wait(bar, 3)

    @pl.when(pos == 0)
    def _():
        pl.semaphore_wait(bar, 2)

    pieces = range(CHUNKS + 1)
    tail = range(CHUNKS + 1 - FORWARDED, CHUNKS + 1)

    def span(ch):
        return pl.ds((ch - 1) * size, size)

    def mine(ch):
        return ids if ch == 0 else own.at[span(ch)]

    def landed(s, ch):
        return row_ids.at[s] if ch == 0 else blocks.at[s, span(ch)]

    def paired(s, ch):
        return pair_ids.at[s] if ch == 0 else blocks.at[s, pl.ds(slots + (ch - 1) * size, size)]

    def along(src, s, ch):
        return pltpu.make_async_remote_copy(
            src_ref=src, dst_ref=landed(s, ch), send_sem=z_send.at[s, ch],
            recv_sem=z_recv.at[s, ch], device_id=(r, ahead), device_id_type=MESH)

    def across(src, s, ch):
        return pltpu.make_async_remote_copy(
            src_ref=src, dst_ref=paired(s, ch), send_sem=p_send.at[s, ch],
            recv_sem=p_recv.at[s, ch], device_id=(partner(s), c), device_id_type=MESH)

    def forward(ch):
        return pltpu.make_async_remote_copy(
            src_ref=paired(pos, ch), dst_ref=paired(pos, ch), send_sem=f_send.at[ch],
            recv_sem=p_recv.at[pos, ch], device_id=(r, ahead), device_id_type=MESH)

    def tile(side, t, what):
        return slab_ids.at[side, t] if what == 0 else slabs.at[side, t, pl.ds(1, slab_slots)]

    def slab_copy(src, side, t, what, to):
        return pltpu.make_async_remote_copy(
            src_ref=src, dst_ref=tile(side, t, what), send_sem=b_send.at[side, t, what],
            recv_sem=b_recv.at[side, t, what], device_id=to, device_id_type=MESH)

    def give(side, t, to, srcs):
        for what in range(2):
            slab_copy(srcs[what], side, t, what, to).start()

    def have(side, t):
        for what in range(2):
            slab_copy(tile(side, t, what), side, t, what, (r, c)).wait_recv()

    def gave(side, t):
        for what in range(2):
            slab_copy(tile(side, t, what), side, t, what, (r, c)).wait_send()

    def tiles(side, t):
        return tile(side, t, 0), tile(side, t, 1)

    block_rows = PANEL // GROUPS

    def returned(g):
        at = pl.ds(pl.multiple_of(g * block_rows * edge, block_rows * edge), block_rows * edge)
        return pltpu.make_async_remote_copy(
            src_ref=result.at[at], dst_ref=result.at[at], send_sem=o_send.at[g],
            recv_sem=o_recv.at[g], device_id=(r, behind), device_id_type=MESH)

    def got(g):
        at = pl.ds(pl.multiple_of(g * block_rows * edge, block_rows * edge), block_rows * edge)
        return pltpu.make_async_remote_copy(
            src_ref=result.at[at], dst_ref=result.at[at], send_sem=o_send.at[g],
            recv_sem=o_recv.at[g], device_id=(r, ahead), device_id_type=MESH)

    plane_two = (shifted(2), c)
    plane_one = (shifted(1), c)
    inward = (r, ahead)
    give(0, 2, plane_two, (names, slab))

    @pl.when(jnp.logical_not(worker))
    def _():
        give(1, 0, inward, (names, slab))
        for ch in range(3):
            along(mine(ch), pos, ch).start()

        @pl.when(pos > 0)
        def _():
            for ch in tail:
                across(mine(ch), pos, ch).start()

        have(0, 2)
        give(1, 2, inward, tiles(0, 2))
        for ch in range(3, CHUNKS + 1):
            along(mine(ch), pos, ch).start()

        @pl.when(pos > 0)
        def _():
            for ch in tail:
                across(mine(ch), pos, ch).wait_recv()
                forward(ch).start()

        for g in range(GROUPS):
            got(g).wait_recv()
            at = pl.ds(g * block_rows * edge, block_rows * edge)
            out[at] = result[at]
        gave(0, 2)
        gave(1, 0)
        gave(1, 2)
        for ch in pieces:
            along(mine(ch), pos, ch).wait_send()

        @pl.when(pos > 0)
        def _():
            for ch in tail:
                across(mine(ch), pos, ch).wait_send()
                forward(ch).wait_send()

    def held_back(s, ch):
        return s == pos + 1 if ch in tail else False

    def send_across(src, s, ch):
        @pl.when(jnp.logical_and(cond_kind(s), jnp.logical_not(held_back(s, ch))))
        def _():
            across(src, s, ch).start()

    def crossed(s, ch):
        waits = cond_kind(s)
        if s == 2 and ch in tail:
            waits = jnp.logical_and(waits, pos != 2)

        @pl.when(waits)
        def _():
            across(landed(s, ch), s, ch).wait_recv()

    def inverted(at_row, at_col, present, base, rows):
        count = at_row.shape[1]
        sub = lax.broadcasted_iota(jnp.int32, (PANEL, count), 0)
        first = lax.broadcasted_iota(jnp.int32, (1, count), 1)
        lane = lax.broadcasted_iota(jnp.int32, (PANEL, 128), 1)
        value = jnp.where(present, first + (1 + base), 0)
        hit = jnp.where(at_col == sub, value, 0)
        found = jnp.zeros((PANEL, 128), jnp.int32)
        for a in range(rows):
            most = jnp.max(jnp.where(at_row == a, hit, 0), axis=1, keepdims=True)
            found = jnp.where(lane == a, most, found)
        return found

    def prepare(s):
        q = partner(s)
        low, high = jnp.minimum(r, q) * PANEL, jnp.maximum(r, q) * PANEL

        def part(ref, base, turn):
            i, j = ref[s, 0] - low, ref[s, 1] - high
            keep = ref[s, 2] > 0
            return inverted(j if turn else i, i if turn else j, keep, base, PANEL)

        @pl.when(r < q)
        def _():
            table[0:PANEL] = jnp.maximum(part(row_ids, 0, False), part(pair_ids, slots, False))

        @pl.when(r > q)
        def _():
            table[0:PANEL] = jnp.maximum(part(row_ids, 0, True), part(pair_ids, slots, True))

        @pl.when(r == q)
        def _():
            i, j = row_ids[s, 0] - low, row_ids[s, 1] - high
            keep = row_ids[s, 2] > 0
            off = jnp.logical_and(keep, i != j)
            table[0:PANEL] = jnp.maximum(
                inverted(i, j, keep, 0, PANEL), inverted(j, i, off, slots, PANEL))

        places = ((0, flipped(s, pos, 2), c), (1, flipped(s, fed, 2), fed_col))
        for side, t, col in places:
            table[(1 + side) * PANEL : (2 + side) * PANEL] = inverted(
                slab_ids[side, t, 1] - col * SLAB, slab_ids[side, t, 0] - q * PANEL,
                slab_ids[side, t, 2] > 0, 0, SLAB)
        fetch = pltpu.make_async_copy(table, scalars.at[s], t_sem.at[0])
        fetch.start()
        fetch.wait()

    def lay_slab(s):
        places = ((0, flipped(s, pos, 2)), (1, flipped(s, fed, 2)))

        def slab_row(k, carry):
            for side, t in places:
                for n in range(SLAB):
                    at = side * width + n * edge
                    right_all[k, :, at : at + edge] = slabs[
                        side, t, scalars[s, (1 + side) * PANEL + k, n]]
            return carry

        lax.fori_loop(0, PANEL, slab_row, 0)

    def move(s, to, of, turn):
        def some(g, carry):
            for x in range(4):
                block = blocks[s, of + g * 4 + x]
                stage[s % 2, 1 + to + g * 4 + x] = block.T if turn else block
            return carry

        lax.fori_loop(0, size // 4, some, 0)

    def hold(s, at):
        turned = r > partner(s)

        @pl.when(turned)
        def _():
            move(s, at, at, True)

        @pl.when(jnp.logical_not(turned))
        def _():
            move(s, at, at, False)

    def hold_row(s, ch):
        at = (ch - 1) * size
        hold(s, at)

        @pl.when(jnp.logical_not(cond_kind(s)))
        def _():
            move(s, slots + at, at, True)

    def hold_pair(s, ch):
        @pl.when(cond_kind(s))
        def _():
            hold(s, slots + (ch - 1) * size)

    depth = PANEL * edge

    def rows_of(g):
        return pl.ds(pl.multiple_of(g * block_rows * edge, block_rows * edge), block_rows * edge)

    def some_rows(s, g, right):
        rows = []
        for a in range(block_rows):
            rows.append(jnp.concatenate(
                [stage[s % 2, scalars[s, j, g * block_rows + a]] for j in range(PANEL)], axis=1))
        return jnp.dot(
            jnp.concatenate(rows, axis=0), right, preferred_element_type=jnp.float32)

    def multiply(s, first, begin, end):
        right = right_all[...].reshape(depth, 2 * width)

        def product(g, carry):
            total = some_rows(s, g, right)
            acc[rows_of(g)] = total if first else total + acc[rows_of(g)]
            return carry

        lax.fori_loop(begin, end, product, 0)

    def tabulate(s):
        crossed(s, 0)
        prepare(s)

    def both(s, *chs):
        for ch in chs:
            hold_row(s, ch)
            crossed(s, ch)
            hold_pair(s, ch)

    @pl.when(worker)
    def _():
        give(0, 1, plane_one, (names, slab))
        for ch in pieces:
            along(mine(ch), pos, ch).start()
        for ch in (0, *tail, *range(1, CHUNKS + 1 - FORWARDED)):
            send_across(mine(ch), pos, ch)
        local = (
            pltpu.make_async_copy(own, blocks.at[pos, pl.ds(0, slots)], l_sem.at[0]),
            pltpu.make_async_copy(ids, row_ids.at[pos], l_sem.at[1]),
            pltpu.make_async_copy(slab, slabs.at[0, 0, pl.ds(1, slab_slots)], l_sem.at[2]),
            pltpu.make_async_copy(names, slab_ids.at[0, 0], l_sem.at[3]),
        )
        for copy in local:
            copy.start()
        zero_block = jnp.zeros((edge, edge), blocks.dtype)
        for side in range(2):
            for t in range(STEPS):
                slabs[side, t, 0] = zero_block
        for n in range(2):
            stage[n, 0] = zero_block

        def relay_fed(ch):
            along(landed(fed, ch), fed, ch).wait_recv()
            along(landed(fed, ch), fed, ch).start()
            send_across(landed(fed, ch), fed, ch)

        for ch in pieces:
            along(landed(near, ch), near, ch).wait_recv()
            send_across(landed(near, ch), near, ch)
            if ch == 1:
                for copy in local:
                    copy.wait()
            if ch == 2:
                have(0, 2)
                give(0, 3, plane_one, tiles(0, 2))
            if ch == 4:
                have(1, 0)
                give(1, 1, plane_one, tiles(1, 0))
            if ch == 6:
                for n in range(3):
                    relay_fed(n)
            if ch >= 2:
                both(1, ch - 1)

        @pl.when(pos == 2)
        def _():
            for ch in tail:
                across(landed(pos, ch), pos, ch).wait_recv()
                forward(ch).start()

        def from_far(ch):
            along(landed(far, ch), far, ch).wait_recv()
            send_across(landed(far, ch), far, ch)

        def pairs(s, *chs):
            for ch in chs:
                crossed(s, ch)
                hold_pair(s, ch)

        half = CHUNKS // 2
        from_far(0)
        both(1, CHUNKS)
        for n in range(1, half + 1):
            hold_row(2, n)
        from_far(1)
        for n in range(half + 1, CHUNKS + 1):
            hold_row(2, n)
        have(1, 2)
        give(1, 3, plane_one, tiles(1, 2))
        from_far(2)
        have(0, 1)
        have(0, 3)
        have(1, 1)
        have(1, 3)
        relay_fed(3)
        tabulate(1)
        lay_slab(1)
        multiply(1, True, 0, 2)
        relay_fed(4)
        from_far(3)
        multiply(1, True, 2, GROUPS)
        tabulate(2)
        relay_fed(5)
        from_far(4)
        pairs(2, *range(1, CHUNKS + 1))
        lay_slab(2)
        relay_fed(6)
        from_far(5)
        multiply(2, False, 0, 2)
        tabulate(0)
        relay_fed(7)
        from_far(6)
        multiply(2, False, 2, GROUPS)
        tabulate(STEPS - 1)
        both(0, 1, 2)
        relay_fed(8)

        @pl.when(pos == 2)
        def _():
            from_far(7)
            from_far(8)

        both(0, *range(3, CHUNKS + 1))
        both(STEPS - 1, 1, 2)

        @pl.when(pos == 1)
        def _():
            from_far(7)

        lay_slab(0)
        multiply(0, False, 0, 2)

        @pl.when(pos == 1)
        def _():
            from_far(8)

        multiply(0, False, 2, GROUPS)
        s = STEPS - 1
        lay_slab(s)
        both(s, *range(3, CHUNKS + 1))
        right = right_all[:, :, width:].reshape(depth, width)

        def last_away(g, carry):
            total = some_rows(s, g, right) + acc[rows_of(g), width:]
            result[rows_of(g)] = total.astype(result.dtype)

            @pl.when(g > 0)
            def _():
                returned(g - 1).start()
            return carry

        lax.fori_loop(0, GROUPS, last_away, 0)
        kept = right_all[:, :, :width].reshape(depth, width)

        def last_here(g, carry):
            total = some_rows(s, g, kept) + acc[rows_of(g), :width]
            out[rows_of(g)] = total.astype(out.dtype)

            @pl.when(g == 0)
            def _():
                returned(GROUPS - 1).start()
            return carry

        lax.fori_loop(0, GROUPS, last_here, 0)
        for t in range(1, STEPS):
            gave(0, t)
        gave(1, 1)
        gave(1, 3)
        for ch in pieces:
            for s in range(STEPS):
                @pl.when(jnp.logical_and(cond_kind(s), jnp.logical_not(held_back(s, ch))))
                def _():
                    across(landed(s, ch), s, ch).wait_send()
            along(landed(pos, ch), pos, ch).wait_send()
            along(landed(fed, ch), fed, ch).wait_send()

        @pl.when(pos == 2)
        def _():
            for ch in tail:
                forward(ch).wait_send()

        for g in range(GROUPS):
            returned(g).wait_send()


def product_call(own, slab, ids, names, stride, bits):
    any_spec = pl.BlockSpec(memory_space=pl.ANY)
    dma = pltpu.SemaphoreType.DMA
    slots, edge = own.shape[0], own.shape[1]
    tile = (PANEL * edge, SLAB * edge)
    listed = pltpu.VMEM((STEPS,) + ids.shape, ids.dtype)
    return pl.pallas_call(
        functools.partial(product_kernel, stride, bits),
        out_shape=jax.ShapeDtypeStruct(tile, own.dtype),
        in_specs=[any_spec] * 4,
        out_specs=pl.BlockSpec(memory_space=pltpu.VMEM),
        scratch_shapes=[
            pltpu.VMEM((STEPS, 2 * slots, edge, edge), own.dtype),
            pltpu.VMEM((2, STEPS, slab.shape[0] + 1, edge, edge), own.dtype),
            listed, listed, pltpu.VMEM((2, STEPS) + names.shape, names.dtype),
            pltpu.VMEM((2, 2 * slots + 1, edge, edge), own.dtype),
            pltpu.VMEM((PANEL, edge, 2 * SLAB * edge), own.dtype),
            pltpu.VMEM((PANEL * edge, 2 * SLAB * edge), jnp.float32),
            pltpu.VMEM(tile, own.dtype),
            pltpu.VMEM((3 * PANEL, 128), jnp.int32),
            pltpu.SMEM((STEPS, 3 * PANEL, 128), jnp.int32),
            dma((STEPS, CHUNKS + 1)), dma((STEPS, CHUNKS + 1)),
            dma((STEPS, CHUNKS + 1)), dma((STEPS, CHUNKS + 1)), dma((CHUNKS + 1,)),
            dma((2, STEPS, 2)), dma((2, STEPS, 2)), dma((GROUPS,)), dma((GROUPS,)),
            dma((4,)), dma((1,)),
        ],
        compiler_params=pltpu.CompilerParams(
            collective_id=0, has_side_effects=True, vmem_limit_bytes=56 * 2**20
        ),
    )(own, slab, ids, names)


def on_device(stored_blocks, stored_ids, slab_blocks, slab_ids, pair_lists):
    stride = lax.axis_size("col") // STEPS
    bits = lax.axis_size("row").bit_length() - 1
    ids = stored_ids.reshape(stored_ids.shape[2], 1, stored_ids.shape[3])
    names = slab_ids.reshape(slab_ids.shape[2], 1, slab_ids.shape[3])
    return product_call(stored_blocks[0, 0], slab_blocks[0, 0], ids, names, stride, bits)


def solution(mesh):
    return jax.shard_map(
        on_device,
        mesh=mesh,
        in_specs=(
            P("row", "col", None, None, None),
            P("row", "col", None, None),
            P("row", "col", None, None, None),
            P("row", "col", None, None),
            P("row", "col", None, None, None),
        ),
        out_specs=P("row", "col"),
        check_vma=False,
    )
```

```python
import functools

import jax
import jax.numpy as jnp
from jax import lax
from jax.experimental import pallas as pl
from jax.experimental.pallas import tpu as pltpu
from jax.sharding import PartitionSpec as P

PANEL = 16
SLAB = 2
STEPS = 4
CHUNKS = 8
FORWARDED = 1
PUT_OFF = 4
GROUPS = 4
MESH = pl.DeviceIdType.MESH


def flipped(value, mask, bits):
    out = value
    for b in range(bits):
        w = 2**b
        out = out + ((mask // w) % 2) * (w - 2 * w * ((value // w) % 2))
    return out


def product_kernel(
    stride, bits, own, slab, ids, names, out, blocks, slabs, row_ids, pair_ids, slab_ids,
    stage, right_all, acc, result, table, scalars,
    z_send, z_recv, p_send, p_recv, f_send, b_send, b_recv, o_send, o_recv, l_sem, t_sem,
):
    r = lax.axis_index("row")
    c = lax.axis_index("col")
    pos = c // stride
    rem = c % stride
    slots, edge = own.shape[0], own.shape[1]
    size = slots // CHUNKS
    slab_slots = slab.shape[0]
    width = SLAB * edge
    worker = jnp.logical_and(pos > 0, pos < STEPS - 1)
    low_side = pos < STEPS // 2
    ahead = jnp.where(low_side, c + stride, c - stride)
    behind = jnp.where(low_side, c - stride, c + stride)
    fed = jnp.where(low_side, 0, STEPS - 1)
    near = STEPS - 1 - pos
    far = STEPS - 1 - fed
    fed_col = jnp.where(worker, behind, c)

    def partner(s):
        return flipped(r, s * stride + rem, bits)

    def shifted(t):
        return flipped(r, t * stride, bits)

    bar = pltpu.get_barrier_semaphore()

    def greet(row, col):
        pl.semaphore_signal(bar, inc=1, device_id=(row, col), device_id_type=MESH)

    def cond_kind(s):
        return s * stride + rem > 0

    greet(r, ahead)
    greet(shifted(2), c)

    @pl.when(worker)
    def _():
        greet(r, behind)
        greet(shifted(1), c)
        for s in range(STEPS):
            @pl.when(cond_kind(s))
            def _():
                greet(partner(s), c)

    @pl.when(pos == STEPS - 1)
    def _():
        greet(partner(STEPS - 1), c)

    @pl.when(worker)
    def _():
        pl.semaphore_wait(bar, 4 + (STEPS - 1) + jnp.minimum(rem, 1))

    @pl.when(pos == STEPS - 1)
    def _():
        pl.semaphore_wait(bar, 3)

    @pl.when(pos == 0)
    def _():
        pl.semaphore_wait(bar, 2)

    pieces = range(CHUNKS + 1)
    tail = range(CHUNKS + 1 - FORWARDED, CHUNKS + 1)

    def span(ch):
        return pl.ds((ch - 1) * size, size)

    def mine(ch):
        return ids if ch == 0 else own.at[span(ch)]

    def landed(s, ch):
        return row_ids.at[s] if ch == 0 else blocks.at[s, span(ch)]

    def paired(s, ch):
        return pair_ids.at[s] if ch == 0 else blocks.at[s, pl.ds(slots + (ch - 1) * size, size)]

    def along(src, s, ch):
        return pltpu.make_async_remote_copy(
            src_ref=src, dst_ref=landed(s, ch), send_sem=z_send.at[s, ch],
            recv_sem=z_recv.at[s, ch], device_id=(r, ahead), device_id_type=MESH)

    def across(src, s, ch):
        return pltpu.make_async_remote_copy(
            src_ref=src, dst_ref=paired(s, ch), send_sem=p_send.at[s, ch],
            recv_sem=p_recv.at[s, ch], device_id=(partner(s), c), device_id_type=MESH)

    def forward(ch):
        return pltpu.make_async_remote_copy(
            src_ref=paired(pos, ch), dst_ref=paired(pos, ch), send_sem=f_send.at[ch],
            recv_sem=p_recv.at[pos, ch], device_id=(r, ahead), device_id_type=MESH)

    def tile(side, t, what):
        return slab_ids.at[side, t] if what == 0 else slabs.at[side, t, pl.ds(1, slab_slots)]

    def slab_copy(src, side, t, what, to):
        return pltpu.make_async_remote_copy(
            src_ref=src, dst_ref=tile(side, t, what), send_sem=b_send.at[side, t, what],
            recv_sem=b_recv.at[side, t, what], device_id=to, device_id_type=MESH)

    def give(side, t, to, srcs):
        for what in range(2):
            slab_copy(srcs[what], side, t, what, to).start()

    def have(side, t):
        for what in range(2):
            slab_copy(tile(side, t, what), side, t, what, (r, c)).wait_recv()

    def gave(side, t):
        for what in range(2):
            slab_copy(tile(side, t, what), side, t, what, (r, c)).wait_send()

    def tiles(side, t):
        return tile(side, t, 0), tile(side, t, 1)

    block_rows = PANEL // GROUPS

    def returned(g):
        at = pl.ds(pl.multiple_of(g * block_rows * edge, block_rows * edge), block_rows * edge)
        return pltpu.make_async_remote_copy(
            src_ref=result.at[at], dst_ref=result.at[at], send_sem=o_send.at[g],
            recv_sem=o_recv.at[g], device_id=(r, behind), device_id_type=MESH)

    def got(g):
        at = pl.ds(pl.multiple_of(g * block_rows * edge, block_rows * edge), block_rows * edge)
        return pltpu.make_async_remote_copy(
            src_ref=result.at[at], dst_ref=result.at[at], send_sem=o_send.at[g],
            recv_sem=o_recv.at[g], device_id=(r, ahead), device_id_type=MESH)

    plane_two = (shifted(2), c)
    plane_one = (shifted(1), c)
    inward = (r, ahead)
    give(0, 2, plane_two, (names, slab))

    @pl.when(jnp.logical_not(worker))
    def _():
        give(1, 0, inward, (names, slab))
        for ch in range(3):
            along(mine(ch), pos, ch).start()

        @pl.when(pos > 0)
        def _():
            for ch in tail:
                across(mine(ch), pos, ch).start()

        have(0, 2)
        give(1, 2, inward, tiles(0, 2))
        for ch in range(3, CHUNKS + 1):
            along(mine(ch), pos, ch).start()

        @pl.when(pos > 0)
        def _():
            for ch in tail:
                across(mine(ch), pos, ch).wait_recv()
                forward(ch).start()

        for g in range(GROUPS):
            got(g).wait_recv()
            at = pl.ds(g * block_rows * edge, block_rows * edge)
            out[at] = result[at]
        gave(0, 2)
        gave(1, 0)
        gave(1, 2)
        for ch in pieces:
            along(mine(ch), pos, ch).wait_send()

        @pl.when(pos > 0)
        def _():
            for ch in tail:
                across(mine(ch), pos, ch).wait_send()
                forward(ch).wait_send()

    def held_back(s, ch):
        return s == pos + 1 if ch in tail else False

    second_core = partner(STEPS - 1) % 2 == 1
    late = range(CHUNKS + 1 - PUT_OFF, CHUNKS + 1)

    def waits_longer(ch):
        if ch == late[0]:
            return jnp.logical_and(second_core, pos == 2)
        return second_core

    def send_across(src, s, ch):
        sends = jnp.logical_and(cond_kind(s), jnp.logical_not(held_back(s, ch)))
        if ch in late:
            put_off = jnp.logical_and(s == STEPS - 1, waits_longer(ch))
            sends = jnp.logical_and(sends, jnp.logical_not(put_off))

        @pl.when(sends)
        def _():
            across(src, s, ch).start()

    def send_late():
        for ch in late:
            @pl.when(jnp.logical_and(waits_longer(ch), jnp.logical_not(held_back(STEPS - 1, ch))))
            def _():
                across(landed(STEPS - 1, ch), STEPS - 1, ch).start()

    def crossed(s, ch):
        waits = cond_kind(s)
        if s == 2 and ch in tail:
            waits = jnp.logical_and(waits, pos != 2)

        @pl.when(waits)
        def _():
            across(landed(s, ch), s, ch).wait_recv()

    def inverted(at_row, at_col, present, base, rows):
        count = at_row.shape[1]
        sub = lax.broadcasted_iota(jnp.int32, (PANEL, count), 0)
        first = lax.broadcasted_iota(jnp.int32, (1, count), 1)
        lane = lax.broadcasted_iota(jnp.int32, (PANEL, 128), 1)
        value = jnp.where(present, first + (1 + base), 0)
        hit = jnp.where(at_col == sub, value, 0)
        found = jnp.zeros((PANEL, 128), jnp.int32)
        for a in range(rows):
            most = jnp.max(jnp.where(at_row == a, hit, 0), axis=1, keepdims=True)
            found = jnp.where(lane == a, most, found)
        return found

    def prepare(s):
        q = partner(s)
        low, high = jnp.minimum(r, q) * PANEL, jnp.maximum(r, q) * PANEL

        def part(ref, base, turn):
            i, j = ref[s, 0] - low, ref[s, 1] - high
            keep = ref[s, 2] > 0
            return inverted(j if turn else i, i if turn else j, keep, base, PANEL)

        @pl.when(r < q)
        def _():
            table[0:PANEL] = jnp.maximum(part(row_ids, 0, False), part(pair_ids, slots, False))

        @pl.when(r > q)
        def _():
            table[0:PANEL] = jnp.maximum(part(row_ids, 0, True), part(pair_ids, slots, True))

        @pl.when(r == q)
        def _():
            i, j = row_ids[s, 0] - low, row_ids[s, 1] - high
            keep = row_ids[s, 2] > 0
            off = jnp.logical_and(keep, i != j)
            table[0:PANEL] = jnp.maximum(
                inverted(i, j, keep, 0, PANEL), inverted(j, i, off, slots, PANEL))

        places = ((0, flipped(s, pos, 2), c), (1, flipped(s, fed, 2), fed_col))
        for side, t, col in places:
            table[(1 + side) * PANEL : (2 + side) * PANEL] = inverted(
                slab_ids[side, t, 1] - col * SLAB, slab_ids[side, t, 0] - q * PANEL,
                slab_ids[side, t, 2] > 0, 0, SLAB)
        fetch = pltpu.make_async_copy(table, scalars.at[s], t_sem.at[0])
        fetch.start()
        fetch.wait()

    def lay_slab(s):
        places = ((0, flipped(s, pos, 2)), (1, flipped(s, fed, 2)))

        def slab_row(k, carry):
            for side, t in places:
                for n in range(SLAB):
                    at = side * width + n * edge
                    right_all[s // 2, k, :, at : at + edge] = slabs[
                        side, t, scalars[s, (1 + side) * PANEL + k, n]]
            return carry

        lax.fori_loop(0, PANEL, slab_row, 0)

    def move(s, to, of, turn):
        def some(g, carry):
            for x in range(4):
                block = blocks[s, of + g * 4 + x]
                stage[s // 2, 1 + to + g * 4 + x] = block.T if turn else block
            return carry

        lax.fori_loop(0, size // 4, some, 0)

    def hold(s, at):
        turned = r > partner(s)

        @pl.when(turned)
        def _():
            move(s, at, at, True)

        @pl.when(jnp.logical_not(turned))
        def _():
            move(s, at, at, False)

    def hold_row(s, ch):
        at = (ch - 1) * size
        hold(s, at)

        @pl.when(jnp.logical_not(cond_kind(s)))
        def _():
            move(s, slots + at, at, True)

    def hold_pair(s, ch):
        @pl.when(cond_kind(s))
        def _():
            hold(s, slots + (ch - 1) * size)

    depth = PANEL * edge

    def rows_of(g):
        return pl.ds(pl.multiple_of(g * block_rows * edge, block_rows * edge), block_rows * edge)

    def some_rows(s, g, right):
        rows = []
        for a in range(block_rows):
            rows.append(jnp.concatenate(
                [stage[s // 2, scalars[s, j, g * block_rows + a]] for j in range(PANEL)], axis=1))
        return jnp.dot(
            jnp.concatenate(rows, axis=0), right, preferred_element_type=jnp.float32)

    def multiply(s, first, begin, end):
        right = right_all[s // 2].reshape(depth, 2 * width)

        def product(g, carry):
            total = some_rows(s, g, right)
            acc[rows_of(g)] = total if first else total + acc[rows_of(g)]
            return carry

        lax.fori_loop(begin, end, product, 0)

    def tabulate(s):
        crossed(s, 0)
        prepare(s)

    def both(s, *chs):
        for ch in chs:
            hold_row(s, ch)
            crossed(s, ch)
            hold_pair(s, ch)

    @pl.when(worker)
    def _():
        give(0, 1, plane_one, (names, slab))
        for ch in pieces:
            along(mine(ch), pos, ch).start()
        for ch in (0, *tail, *range(1, CHUNKS + 1 - FORWARDED)):
            send_across(mine(ch), pos, ch)
        local = (
            pltpu.make_async_copy(own, blocks.at[pos, pl.ds(0, slots)], l_sem.at[0]),
            pltpu.make_async_copy(ids, row_ids.at[pos], l_sem.at[1]),
            pltpu.make_async_copy(slab, slabs.at[0, 0, pl.ds(1, slab_slots)], l_sem.at[2]),
            pltpu.make_async_copy(names, slab_ids.at[0, 0], l_sem.at[3]),
        )
        for copy in local:
            copy.start()
        zero_block = jnp.zeros((edge, edge), blocks.dtype)
        for side in range(2):
            for t in range(STEPS):
                slabs[side, t, 0] = zero_block
        for n in range(2):
            stage[n, 0] = zero_block

        def relay_fed(ch):
            along(landed(fed, ch), fed, ch).wait_recv()
            along(landed(fed, ch), fed, ch).start()
            send_across(landed(fed, ch), fed, ch)

        for ch in pieces:
            along(landed(near, ch), near, ch).wait_recv()
            send_across(landed(near, ch), near, ch)
            if ch == 1:
                for copy in local:
                    copy.wait()
            if ch == 2:
                have(0, 2)
                give(0, 3, plane_one, tiles(0, 2))
            if ch == 4:
                have(1, 0)
                give(1, 1, plane_one, tiles(1, 0))
            if ch == 6:
                for n in range(3):
                    relay_fed(n)
            if ch >= 2:
                both(1, ch - 1)

        @pl.when(pos == 2)
        def _():
            for ch in tail:
                across(landed(pos, ch), pos, ch).wait_recv()
                forward(ch).start()

        def from_far(ch):
            along(landed(far, ch), far, ch).wait_recv()
            send_across(landed(far, ch), far, ch)

        def pairs(s, *chs):
            for ch in chs:
                crossed(s, ch)
                hold_pair(s, ch)

        half = CHUNKS // 2
        from_far(0)
        both(1, CHUNKS)
        for n in range(1, half + 1):
            hold_row(2, n)
        from_far(1)
        for n in range(half + 1, CHUNKS + 1):
            hold_row(2, n)
        have(1, 2)
        give(1, 3, plane_one, tiles(1, 2))
        from_far(2)
        have(0, 1)
        have(0, 3)
        have(1, 1)
        have(1, 3)
        relay_fed(3)
        tabulate(1)
        lay_slab(1)
        multiply(1, True, 0, 2)
        relay_fed(4)
        from_far(3)
        multiply(1, True, 2, GROUPS)
        tabulate(2)
        relay_fed(5)
        from_far(4)
        pairs(2, *range(1, CHUNKS + 1))
        lay_slab(2)
        both(0, 1, 2)
        relay_fed(6)
        from_far(5)
        multiply(2, False, 0, 2)
        tabulate(0)
        both(0, 3)
        relay_fed(7)
        from_far(6)
        multiply(2, False, 2, GROUPS)
        tabulate(STEPS - 1)
        both(0, 4)
        relay_fed(8)

        @pl.when(pos == 2)
        def _():
            send_late()

        lay_slab(0)
        lay_slab(STEPS - 1)
        both(0, 5, 6)
        from_far(7)
        both(0, 7)
        both(STEPS - 1, 1, 2)
        for n in range(3, 7):
            hold_row(STEPS - 1, n)

        @pl.when(pos == 2)
        def _():
            from_far(8)

        both(0, 8)

        def away(s):
            return right_all[s // 2][:, :, width:].reshape(depth, width)

        def first_away(g, carry):
            acc[rows_of(g), width:] += some_rows(0, g, away(0))
            return carry

        lax.fori_loop(0, GROUPS, first_away, 0)

        @pl.when(pos == 1)
        def _():
            from_far(8)
            send_late()

        s = STEPS - 1
        pairs(s, *range(3, 7))
        both(s, 7, 8)

        def last_away(g, carry):
            total = some_rows(s, g, away(s)) + acc[rows_of(g), width:]
            result[rows_of(g)] = total.astype(result.dtype)

            @pl.when(g > 0)
            def _():
                returned(g - 1).start()
            return carry

        lax.fori_loop(0, GROUPS, last_away, 0)

        def here(s):
            return right_all[s // 2][:, :, :width].reshape(depth, width)

        def last_here(g, carry):
            total = some_rows(s, g, here(s)) + acc[rows_of(g), :width]
            total = total + some_rows(0, g, here(0))
            out[rows_of(g)] = total.astype(out.dtype)

            @pl.when(g == 0)
            def _():
                returned(GROUPS - 1).start()
            return carry

        lax.fori_loop(0, GROUPS, last_here, 0)
        for t in range(1, STEPS):
            gave(0, t)
        gave(1, 1)
        gave(1, 3)
        for ch in pieces:
            for s in range(STEPS):
                @pl.when(jnp.logical_and(cond_kind(s), jnp.logical_not(held_back(s, ch))))
                def _():
                    across(landed(s, ch), s, ch).wait_send()
            along(landed(pos, ch), pos, ch).wait_send()
            along(landed(fed, ch), fed, ch).wait_send()

        @pl.when(pos == 2)
        def _():
            for ch in tail:
                forward(ch).wait_send()

        for g in range(GROUPS):
            returned(g).wait_send()


def product_call(own, slab, ids, names, stride, bits):
    any_spec = pl.BlockSpec(memory_space=pl.ANY)
    dma = pltpu.SemaphoreType.DMA
    slots, edge = own.shape[0], own.shape[1]
    tile = (PANEL * edge, SLAB * edge)
    listed = pltpu.VMEM((STEPS,) + ids.shape, ids.dtype)
    return pl.pallas_call(
        functools.partial(product_kernel, stride, bits),
        out_shape=jax.ShapeDtypeStruct(tile, own.dtype),
        in_specs=[any_spec] * 4,
        out_specs=pl.BlockSpec(memory_space=pltpu.VMEM),
        scratch_shapes=[
            pltpu.VMEM((STEPS, 2 * slots, edge, edge), own.dtype),
            pltpu.VMEM((2, STEPS, slab.shape[0] + 1, edge, edge), own.dtype),
            listed, listed, pltpu.VMEM((2, STEPS) + names.shape, names.dtype),
            pltpu.VMEM((2, 2 * slots + 1, edge, edge), own.dtype),
            pltpu.VMEM((2, PANEL, edge, 2 * SLAB * edge), own.dtype),
            pltpu.VMEM((PANEL * edge, 2 * SLAB * edge), jnp.float32),
            pltpu.VMEM(tile, own.dtype),
            pltpu.VMEM((3 * PANEL, 128), jnp.int32),
            pltpu.SMEM((STEPS, 3 * PANEL, 128), jnp.int32),
            dma((STEPS, CHUNKS + 1)), dma((STEPS, CHUNKS + 1)),
            dma((STEPS, CHUNKS + 1)), dma((STEPS, CHUNKS + 1)), dma((CHUNKS + 1,)),
            dma((2, STEPS, 2)), dma((2, STEPS, 2)), dma((GROUPS,)), dma((GROUPS,)),
            dma((4,)), dma((1,)),
        ],
        compiler_params=pltpu.CompilerParams(
            collective_id=0, has_side_effects=True, vmem_limit_bytes=56 * 2**20
        ),
    )(own, slab, ids, names)


def on_device(stored_blocks, stored_ids, slab_blocks, slab_ids, pair_lists):
    stride = lax.axis_size("col") // STEPS
    bits = lax.axis_size("row").bit_length() - 1
    ids = stored_ids.reshape(stored_ids.shape[2], 1, stored_ids.shape[3])
    names = slab_ids.reshape(slab_ids.shape[2], 1, slab_ids.shape[3])
    return product_call(stored_blocks[0, 0], slab_blocks[0, 0], ids, names, stride, bits)


def solution(mesh):
    return jax.shard_map(
        on_device,
        mesh=mesh,
        in_specs=(
            P("row", "col", None, None, None),
            P("row", "col", None, None),
            P("row", "col", None, None, None),
            P("row", "col", None, None),
            P("row", "col", None, None, None),
        ),
        out_specs=P("row", "col"),
        check_vma=False,
    )
```
